32 devices in a mesh: groups: 2 (over y), img: 4 (over z), ref: 2 (over x), rep: 2 (over core).
Axes of the slice: x: 2, y: 2, z: 4, core: 2. Of those that a mesh axis runs over, the one named last changes fastest.
Arguments:
- images: float32 [768, 4096], P(('groups', 'img')), parts along dimension 0, may hold values from -24 to 24
- references: float32 [4096, 2048], P('img', ('groups', 'ref', 'rep')), parts along dimension 1, may hold values from -1.2 to 1.2
- rotations: int32 [2048], P(('groups', 'ref', 'rep')), parts along dimension 0, may hold values from 0 to 7
- image_group: int32 [768], P(('groups', 'img')), parts along dimension 0, may hold values from 0 to 15
- noise_var: float32 [16], replicated, may hold values from 0.5 to 2
Outputs:
- class_means: float32 [4096, 2048], P('img', ('groups', 'ref', 'rep')), parts along dimension 1
- class_weights: float32 [2048], P(('groups', 'ref', 'rep')), parts along dimension 0
- log_evidence: float32 [768], P(('groups', 'img')), parts along dimension 0
The draws below stay inside these ranges and needn't reach their ends.
There are 2 independent parts, one for each index of `groups`. The reference program is written for one: setup_inputs(seed, part) draws one part's arguments, and reference() takes and returns one part's arrays. A program takes and returns all parts, laid end to end along the dimension named above; an argument that names none is the same for every part. Nothing has to cross between parts.
All inputs are finite; a program needn't handle non-finite values.
Results may differ from the reference program's by a relative error of at most 0.0003.
Values sent between devices are 32-bit elements; how exact they have to be, the bound alone decides.
A program may use at most 64 MiB of HBM per device.

```python
import math
import jax
import jax.numpy as jnp
from jax import lax

IMAGE_SIDE = 64
PIXELS = 4096
CLASSES = 1024
IMAGES = 384
NOISE_GROUPS = 16


def shared_classes(key):
    values = jax.random.normal(jax.random.fold_in(key, 101), (PIXELS, CLASSES), jnp.float32)
    scales = jnp.full((CLASSES,), 0.05, jnp.float32)
    values = jnp.clip(values, -6.0, 6.0) * scales[None, :]
    turns = jax.random.randint(jax.random.fold_in(key, 103), (CLASSES,), 0, 8).astype(jnp.int32)
    return (values, turns)


def draw_references(key, part):
    return shared_classes(key)[0]


def draw_rotations(key, part):
    return shared_classes(key)[1]


def draw_images(key, part):
    base = jnp.clip(jax.random.normal(jax.random.fold_in(key, 301), (IMAGES, PIXELS), jnp.float32), -6.0, 6.0)
    return jnp.clip(base, -24.0, 24.0)


def touch_ends(values, own_key, low, top_value):
    index_at = [jax.random.randint(jax.random.fold_in(own_key, axis), (), 0, length) for axis, length in enumerate(values.shape)]
    widest = values.shape.index(max(values.shape))
    beside = index_at[:widest] + [(index_at[widest] + 1) % values.shape[widest]] + index_at[widest + 1:]
    return values.at[tuple(index_at)].set(low).at[tuple(beside)].set(top_value)


def setup_inputs(seed: int = 0, part: int = 0) -> dict:
    seeds = jax.random.split(jax.random.key(seed), 6)
    part_splits = jax.random.split(jax.random.fold_in(seeds[5], part), 6)
    return {
        "images": draw_images(jax.random.fold_in(jax.random.fold_in(seeds[5], part), 71), part),
        "references": draw_references(jax.random.fold_in(jax.random.fold_in(seeds[5], part), 71), part),
        "rotations": draw_rotations(jax.random.fold_in(jax.random.fold_in(seeds[5], part), 71), part),
        "image_group": touch_ends(jax.random.randint(part_splits[3], (IMAGES,), 0, NOISE_GROUPS), jax.random.fold_in(part_splits[3], 1), 0, NOISE_GROUPS - 1).astype(jnp.int32),
        "noise_var": jnp.clip(jnp.exp(jax.random.uniform(seeds[4], (NOISE_GROUPS,), jnp.float32, math.log(0.5), math.log(2.0))), 0.5, 2.0),
    }


def turn_forward(field, which):
    quarter = which % 4
    base = field if which < 4 else jnp.swapaxes(field, 0, 1)
    return jnp.rot90(base, quarter, axes=(0, 1))


def turn_inverse(field, which):
    quarter = which % 4
    base = jnp.rot90(field, -quarter, axes=(0, 1))
    return base if which < 4 else jnp.swapaxes(base, 0, 1)


def select_turn(field, rotations, turner):
    result = jnp.zeros_like(field)
    for which in range(8):
        result = jnp.where(rotations[None, None, :] == which, turner(field, which), result)
    return result


def reference(images, references, rotations, image_group, noise_var):
    rotated = select_turn(references.reshape(IMAGE_SIDE, IMAGE_SIDE, -1), rotations, turn_inverse).reshape(PIXELS, -1)
    norms = jnp.sum(references * references, axis=0)
    sigma = noise_var[image_group]
    scores = (jnp.dot(images, rotated, precision=lax.Precision.HIGHEST, preferred_element_type=jnp.float32) - 0.5 * norms[None, :]) / sigma[:, None]
    top = jnp.max(scores, axis=1)
    log_evidence = top + jnp.log(jnp.sum(jnp.exp(scores - top[:, None]), axis=1))
    posterior = jnp.exp(scores - log_evidence[:, None])
    weight_sum = jnp.sum(posterior, axis=0)
    numer_image = jnp.dot(images.T, posterior, precision=lax.Precision.HIGHEST, preferred_element_type=jnp.float32)
    numerator = select_turn(numer_image.reshape(IMAGE_SIDE, IMAGE_SIDE, -1), rotations, turn_forward).reshape(PIXELS, -1)
    class_means = numerator / (weight_sum + 1.0)[None, :]
    class_weights = weight_sum * (CLASSES / IMAGES)
    return class_means, class_weights, log_evidence
```

```python
import functools

import jax
import jax.numpy as jnp
from jax import lax
from jax.experimental import pallas as pl
from jax.experimental.pallas import tpu as pltpu
from jax.sharding import PartitionSpec as P

IMAGE_SIDE = 64
PIXELS = 4096
MESH = pl.DeviceIdType.MESH
F32 = jnp.float32
BF16 = jnp.bfloat16
CHUNKS = 4
LANES = 128


def joined(part, axis, combine):
    gathered = jax.tree.map(lambda a: lax.all_gather(a, axis), part)

    def take(source):
        return jax.tree.map(lambda a: lax.dynamic_index_in_dim(a, source, 0, False), gathered)

    return lax.fori_loop(
        1, lax.axis_size(axis), lambda source, state: combine(state, take(source)), take(0)
    )


def turn_forward(field, which):
    quarter = which % 4
    base = field if which < 4 else jnp.swapaxes(field, 0, 1)
    return jnp.rot90(base, quarter, axes=(0, 1))


def turn_inverse(field, which):
    quarter = which % 4
    base = jnp.rot90(field, -quarter, axes=(0, 1))
    return base if which < 4 else jnp.swapaxes(base, 0, 1)


def select_turn(field, rotations, turner):
    result = jnp.zeros_like(field)
    for which in range(8):
        result = jnp.where(rotations[None, None, :] == which, turner(field, which), result)
    return result


def combine_stats(first, second):
    top = jnp.maximum(first[0], second[0])
    total = first[1] * jnp.exp(first[0] - top) + second[1] * jnp.exp(second[0] - top)
    return (top, total)


def body(images, references, rotations, image_group, noise_var):
    gathered = lax.all_gather(references, "img", axis=0, tiled=True)
    rotated = select_turn(
        gathered.reshape(IMAGE_SIDE, IMAGE_SIDE, -1), rotations, turn_inverse
    ).reshape(PIXELS, -1)
    norms = jnp.sum(gathered * gathered, axis=0)
    group_hot = image_group[:, None] == jnp.arange(noise_var.shape[0])[None, :]
    sigma = jnp.sum(jnp.where(group_hot, noise_var[None, :], 0.0), axis=1)
    scores = (
        jnp.dot(
            images, rotated, precision=lax.Precision.HIGHEST, preferred_element_type=jnp.float32
        )
        - 0.5 * norms[None, :]
    ) / sigma[:, None]
    local_top = jnp.max(scores, axis=1)
    local_total = jnp.sum(jnp.exp(scores - local_top[:, None]), axis=1)
    top, total = joined((local_top, local_total), ("ref", "rep"), combine_stats)
    log_evidence = top + jnp.log(total)
    posterior = jnp.exp(scores - log_evidence[:, None])
    weight_sum = lax.psum(jnp.sum(posterior, axis=0), "img")
    numer_image = lax.dot_general(
        images,
        posterior,
        (((0,), (0,)), ((), ())),
        precision=lax.Precision.HIGHEST,
        preferred_element_type=jnp.float32,
    )
    numerator = select_turn(
        numer_image.reshape(IMAGE_SIDE, IMAGE_SIDE, -1), rotations, turn_forward
    ).reshape(PIXELS, -1)
    owned = lax.psum_scatter(numerator, "img", scatter_dimension=0, tiled=True)
    class_means = owned / (weight_sum + 1.0)[None, :]
    class_total = weight_sum.shape[0] * lax.axis_size("ref") * lax.axis_size("rep")
    image_total = images.shape[0] * lax.axis_size("img")
    class_weights = weight_sum * (class_total / image_total)
    return (class_means, class_weights, log_evidence)


def halves(x):
    high = x.astype(BF16)
    return high, (x - high.astype(F32)).astype(BF16)


def dot3(a, b, dims):
    ah, al = halves(a)
    bh, bl = halves(b)
    one = lambda x, y: lax.dot_general(x, y, (dims, ((), ())), preferred_element_type=F32)
    return one(ah, bh) + (one(ah, bl) + one(al, bh))


def reverse_rows(x):
    place = lax.broadcasted_iota(jnp.int32, (8, x.shape[1]), 0)
    odd = place % 2 == 1
    second = (place // 2) % 2 == 1
    pieces = []
    for g in reversed(range(x.shape[0] // 8)):
        p = x[8 * g : 8 * g + 8]
        p = jnp.where(odd, pltpu.roll(p, 1, 0), pltpu.roll(p, 7, 0))
        p = jnp.where(second, pltpu.roll(p, 2, 0), pltpu.roll(p, 6, 0))
        pieces.append(pltpu.roll(p, 4, 0))
    return jnp.concatenate(pieces, axis=0)


def kernel(
    zs,
    images_ref, refs_ref, rot_ref, sigma_ref,
    means_ref, weights_ref, evidence_ref,
    full, wide, scores, parts, stats, posts, num,
    load_sem, z_recv, x_recv, c_recv, cx_recv,
    right_send, left_send, x_send, c_send, cx_send,
    s_send, s_recv, t_send, t_recv, p_send, p_recv,
):
    z = lax.axis_index("img")
    x = lax.axis_index("ref")
    c = lax.axis_index("rep")
    rows = images_ref.shape[0]
    classes = refs_ref.shape[1]
    quarter = rows // 4
    strip = PIXELS // CHUNKS
    side = IMAGE_SIDE
    own_lines = side // zs
    others = [{"ref": 1 - x}, {"rep": 1 - c}, {"ref": 1 - x, "rep": 1 - c}]

    barrier = pltpu.get_barrier_semaphore()
    for d in range(1, zs):
        pl.semaphore_signal(barrier, inc=1, device_id={"img": lax.rem(z + d, zs)}, device_id_type=MESH)
    for where in others:
        pl.semaphore_signal(barrier, inc=1, device_id=where, device_id_type=MESH)
    pl.semaphore_wait(barrier, zs + 2)

    def quarter_rows(xi, ci):
        return pl.ds(pl.multiple_of((xi * 2 + ci) * quarter, 8), quarter)

    def columns(chunk):
        return pl.ds(pl.multiple_of(chunk * strip, strip), strip)

    def send(src, dst, ssem, rsem, where):
        return pltpu.make_async_remote_copy(
            src_ref=src, dst_ref=dst, send_sem=ssem, recv_sem=rsem,
            device_id=where, device_id_type=MESH,
        )

    def piece(src, chunk, xi, ci):
        return full.at[src, quarter_rows(xi, ci), columns(chunk)]

    def go_right(src, chunk, first=False):
        a = images_ref.at[quarter_rows(x, c), columns(chunk)] if first else piece(src, chunk, x, c)
        return send(a, piece(src, chunk, x, c), right_send.at[src, chunk], z_recv.at[src, chunk], {"img": lax.rem(z + 1, zs)})

    def go_left(src, chunk, first=False):
        a = images_ref.at[quarter_rows(x, c), columns(chunk)] if first else piece(src, chunk, x, c)
        return send(a, piece(src, chunk, x, c), left_send.at[src, chunk], z_recv.at[src, chunk], {"img": lax.rem(z + zs - 1, zs)})

    def go_x(src, chunk):
        return send(piece(src, chunk, x, c), piece(src, chunk, x, c), x_send.at[src, chunk], x_recv.at[src, chunk], {"ref": 1 - x})

    def go_c(src, chunk):
        return send(piece(src, chunk, x, c), piece(src, chunk, x, c), c_send.at[src, chunk], c_recv.at[src, chunk], {"rep": 1 - c})

    def go_cx(src, chunk):
        return send(piece(src, chunk, 1 - x, c), piece(src, chunk, 1 - x, c), cx_send.at[src, chunk], cx_recv.at[src, chunk], {"rep": 1 - c})

    def partial(src):
        return send(scores.at[src], parts.at[z], s_send.at[src], s_recv.at[z], {"img": src})

    load = pltpu.make_async_copy(images_ref, full.at[z], load_sem)
    load.start()
    for chunk in range(CHUNKS):
        @pl.when(z < zs - 1)
        def _():
            go_right(z, chunk, True).start()

        @pl.when(z > 0)
        def _():
            go_left(z, chunk, True).start()

    rot = rot_ref[...]
    is_row = (rot == 0) | (rot == 7)
    is_row_up = (rot == 5) | (rot == 2)
    is_col = (rot == 4) | (rot == 3)
    is_col_up = (rot == 1) | (rot == 6)
    flipped = (rot == 7) | (rot == 2) | (rot == 3) | (rot == 6)

    def clear(i, _):
        wide[:, pl.ds(pl.multiple_of(i * side, side), side), :] = jnp.zeros((classes // LANES, side, LANES), F32)
        return 0

    lax.fori_loop(0, side, clear, 0)

    def lane(h):
        return slice(h * LANES, (h + 1) * LANES)

    def line(i):
        return pl.ds(pl.multiple_of(i * side, side), side)

    def turned(i):
        field = refs_ref[line(i), :]
        return jnp.where(flipped, reverse_rows(field), field)

    def put_rows(i, norm):
        raw = refs_ref[line(i), :]
        field = turned(i)
        up = jnp.where(is_row, field, 0.0)
        down = jnp.where(is_row_up, field, 0.0)
        for h in range(classes // LANES):
            wide[h, line(z * own_lines + i), :] = up[:, lane(h)]
            wide[h, line(side - 1 - z * own_lines - i), :] = down[:, lane(h)]
        return norm + jnp.sum(raw * raw, axis=0, keepdims=True)

    norm = lax.fori_loop(0, own_lines, put_rows, jnp.zeros((1, classes), F32))

    def put_columns(i, _):
        field = turned(i)
        across = jnp.where(is_col, field, 0.0)
        back = jnp.where(is_col_up, field, 0.0)
        for h in range(classes // LANES):
            at = pl.ds(z * own_lines + i, side, stride=side)
            wide[h, at, :] = wide[h, at, :] + across[:, lane(h)]
            at = pl.ds(side - 1 - z * own_lines - i, side, stride=side)
            wide[h, at, :] = wide[h, at, :] + back[:, lane(h)]
        return 0

    lax.fori_loop(0, own_lines, put_columns, 0)

    def multiply(src, chunk, width):
        at = pl.ds(pl.multiple_of(chunk * width, width), width)
        weight = jnp.concatenate([wide[h, at, :] for h in range(classes // LANES)], axis=1)
        return jnp.dot(full[src, :, at], weight, precision=lax.Precision.HIGHEST, preferred_element_type=F32)

    start = jnp.broadcast_to(-0.5 * norm, (rows, classes))
    for src in range(zs):
        scores[src] = start
    load.wait()

    def own_part(chunk, _):
        scores[z] = scores[z] + multiply(z, chunk, strip)
        return 0

    lax.fori_loop(0, CHUNKS, own_part, 0)

    units = (zs - 1) * CHUNKS

    def each(n, action):
        s = 1 + n // CHUNKS
        chunk = lax.rem(n, CHUNKS)
        good = (n >= 0) & (n < units)

        @pl.when(good & (z - s >= 0))
        def _():
            action(z - s, chunk, True)

        @pl.when(good & (z + s <= zs - 1))
        def _():
            action(z + s, chunk, False)

    def take_z(src, chunk, rightward):
        go_right(src, chunk).wait_recv()
        if rightward:
            @pl.when(z < zs - 1)
            def _():
                go_right(src, chunk).start()
        else:
            @pl.when(z > 0)
            def _():
                go_left(src, chunk).start()
        go_x(src, chunk).start()
        go_c(src, chunk).start()

    def take_x(src, chunk, rightward):
        go_x(src, chunk).wait_recv()
        go_cx(src, chunk).start()

    def take_all(src, chunk, rightward):
        go_c(src, chunk).wait_recv()
        go_cx(src, chunk).wait_recv()
        scores[src] = scores[src] + multiply(src, chunk, strip)

        @pl.when(chunk == CHUNKS - 1)
        def _():
            partial(src).start()

    def unit(n, _):
        each(n, take_z)
        each(n - 1, take_x)
        each(n - 2, take_all)
        return 0

    lax.fori_loop(0, units + 2, unit, 0)

    total_score = scores[z]
    for d in range(1, zs):
        src = lax.rem(z + d, zs)
        send(scores.at[src], parts.at[src], s_send.at[src], s_recv.at[src], {"img": src}).wait_recv()
        total_score = total_score + parts[src]
    total_score = total_score / sigma_ref[...]
    top = jnp.max(total_score, axis=1, keepdims=True)
    total = jnp.sum(jnp.exp(total_score - top), axis=1, keepdims=True)
    place = lax.broadcasted_iota(jnp.int32, (rows, LANES), 1)
    stats[3] = jnp.where(place < LANES // 2, top, total)
    shares = [send(stats.at[3], stats.at[m], t_send.at[m], t_recv.at[m], where) for m, where in enumerate(others)]
    for share in shares:
        share.start()
    for share in shares:
        share.wait()
    half = LANES // 2
    best = top
    for m in range(3):
        best = jnp.maximum(best, stats[m, :, 0:1])
    summed = total * jnp.exp(top - best)
    for m in range(3):
        summed = summed + stats[m, :, half : half + 1] * jnp.exp(stats[m, :, 0:1] - best)
    evidence = best + jnp.log(summed)
    evidence_ref[...] = evidence
    posts[z] = jnp.exp(total_score - evidence)

    def give(src):
        return send(posts.at[z], posts.at[z], p_send.at[src], p_recv.at[z], {"img": src})

    for d in range(1, zs):
        give(lax.rem(z + d, zs)).start()
    for d in range(1, zs):
        src = lax.rem(z + d, zs)
        send(posts.at[src], posts.at[src], p_send.at[src], p_recv.at[src], {"img": src}).wait_recv()

    weight_sum = jnp.zeros((1, classes), F32)
    for src in range(zs):
        weight_sum = weight_sum + jnp.sum(posts[src], axis=0, keepdims=True)
    weights_ref[...] = weight_sum
    width = 512

    def weigh(n, _):
        at = pl.ds(pl.multiple_of(n * width, width), width)
        block = full[:, :, at].reshape(zs * rows, width)
        result = dot3(block, posts[...].reshape(zs * rows, classes), (((0,), (0,))))
        for h in range(classes // LANES):
            num[h, at, :] = result[:, lane(h)]
        return 0

    lax.fori_loop(0, PIXELS // width, weigh, 0)

    scale = 1.0 / (weight_sum + 1.0)

    def finish(i, _):
        fields = []
        for h in range(classes // LANES):
            up = num[h, line(z * own_lines + i), :]
            down = num[h, line(side - 1 - z * own_lines - i), :]
            across = num[h, pl.ds(z * own_lines + i, side, stride=side), :]
            back = num[h, pl.ds(side - 1 - z * own_lines - i, side, stride=side), :]
            k = lane(h)
            fields.append(jnp.where(is_row[:, k], up, jnp.where(is_row_up[:, k], down, jnp.where(is_col[:, k], across, back))))
        field = jnp.concatenate(fields, axis=1)
        means_ref[line(i), :] = jnp.where(flipped, reverse_rows(field), field) * scale
        return 0

    lax.fori_loop(0, own_lines, finish, 0)

    def settle(src, chunk, rightward):
        if rightward:
            @pl.when(z < zs - 1)
            def _():
                go_right(src, chunk).wait_send()
        else:
            @pl.when(z > 0)
            def _():
                go_left(src, chunk).wait_send()
        go_x(src, chunk).wait_send()
        go_c(src, chunk).wait_send()
        go_cx(src, chunk).wait_send()

    def settle_unit(n, _):
        each(n, settle)
        return 0

    lax.fori_loop(0, units, settle_unit, 0)
    for chunk in range(CHUNKS):
        @pl.when(z < zs - 1)
        def _():
            go_right(z, chunk, True).wait_send()

        @pl.when(z > 0)
        def _():
            go_left(z, chunk, True).wait_send()
    for d in range(1, zs):
        src = lax.rem(z + d, zs)
        partial(src).wait_send()
        give(src).wait_send()


def turned_images_body(zs, images, references, rotations, image_group, noise_var):
    rows = images.shape[0]
    pixels, classes = references.shape
    group_hot = image_group[:, None] == jnp.arange(noise_var.shape[0])[None, :]
    sigma = jnp.sum(jnp.where(group_hot, noise_var[None, :], 0.0), axis=1, keepdims=True)
    dma = pltpu.SemaphoreType.DMA
    vmem = pl.BlockSpec(memory_space=pltpu.VMEM)
    many = dma((zs, CHUNKS))
    means, weight_sum, evidence = pl.pallas_call(
        functools.partial(kernel, zs),
        name="class_step",
        out_shape=(
            jax.ShapeDtypeStruct((pixels, classes), F32),
            jax.ShapeDtypeStruct((1, classes), F32),
            jax.ShapeDtypeStruct((rows, 1), F32),
        ),
        in_specs=[pl.BlockSpec(memory_space=pl.ANY), vmem, vmem, vmem],
        out_specs=(vmem, vmem, vmem),
        scratch_shapes=[
            pltpu.VMEM((zs, rows, PIXELS), F32),
            pltpu.VMEM((classes // LANES, PIXELS, LANES), F32),
            pltpu.VMEM((zs, rows, classes), F32),
            pltpu.VMEM((zs, rows, classes), F32),
            pltpu.VMEM((4, rows, LANES), F32),
            pltpu.VMEM((zs, rows, classes), F32),
            pltpu.VMEM((classes // LANES, PIXELS, LANES), F32),
            dma, many, many, many, many, many, many, many, many, many,
            dma((zs,)), dma((zs,)), dma((3,)), dma((3,)), dma((zs,)), dma((zs,)),
        ],
        compiler_params=pltpu.CompilerParams(
            collective_id=0, has_side_effects=True, vmem_limit_bytes=48 * 1024 * 1024
        ),
    )(images, references, rotations[None, :], sigma)
    weight_sum = weight_sum[0]
    class_total = classes * lax.axis_size("ref") * lax.axis_size("rep")
    image_total = rows * zs
    return (means, weight_sum * (class_total / image_total), evidence[:, 0])


def solution(mesh):
    sizes = dict(mesh.shape)
    placed = (
        P(("groups", "img"), None),
        P("img", ("groups", "ref", "rep")),
        P(("groups", "ref", "rep")),
        P(("groups", "img")),
        P(),
    )

    def choose(images, references, rotations, image_group, noise_var):
        zs = sizes["img"]
        rows = images.shape[0]
        fits = (
            sizes["ref"] == 2
            and sizes["rep"] == 2
            and zs % 2 == 0
            and rows % 32 == 0
            and references.shape[1] % LANES == 0
            and IMAGE_SIDE % zs == 0
            and zs * rows * PIXELS * 4 <= 12 * 1024 * 1024
        )
        if fits:
            return turned_images_body(zs, images, references, rotations, image_group, noise_var)
        return body(images, references, rotations, image_group, noise_var)

    return jax.shard_map(
        choose,
        mesh=mesh,
        in_specs=placed,
        out_specs=(
            P("img", ("groups", "ref", "rep")),
            P(("groups", "ref", "rep")),
            P(("groups", "img")),
        ),
        check_vma=False,
    )
```

```python
import functools

import jax
import jax.numpy as jnp
from jax import lax
from jax.experimental import pallas as pl
from jax.experimental.pallas import tpu as pltpu
from jax.sharding import PartitionSpec as P

IMAGE_SIDE = 64
PIXELS = 4096
MESH = pl.DeviceIdType.MESH
F32 = jnp.float32
BF16 = jnp.bfloat16
CHUNKS = 2
LANES = 128
VMEM_BYTES = 62 * 1024 * 1024


def joined(part, axis, combine):
    gathered = jax.tree.map(lambda a: lax.all_gather(a, axis), part)

    def take(source):
        return jax.tree.map(lambda a: lax.dynamic_index_in_dim(a, source, 0, False), gathered)

    return lax.fori_loop(
        1, lax.axis_size(axis), lambda source, state: combine(state, take(source)), take(0)
    )


def turn_forward(field, which):
    quarter = which % 4
    base = field if which < 4 else jnp.swapaxes(field, 0, 1)
    return jnp.rot90(base, quarter, axes=(0, 1))


def turn_inverse(field, which):
    quarter = which % 4
    base = jnp.rot90(field, -quarter, axes=(0, 1))
    return base if which < 4 else jnp.swapaxes(base, 0, 1)


def select_turn(field, rotations, turner):
    result = jnp.zeros_like(field)
    for which in range(8):
        result = jnp.where(rotations[None, None, :] == which, turner(field, which), result)
    return result


def combine_stats(first, second):
    top = jnp.maximum(first[0], second[0])
    total = first[1] * jnp.exp(first[0] - top) + second[1] * jnp.exp(second[0] - top)
    return (top, total)


def body(images, references, rotations, image_group, noise_var):
    gathered = lax.all_gather(references, "img", axis=0, tiled=True)
    rotated = select_turn(
        gathered.reshape(IMAGE_SIDE, IMAGE_SIDE, -1), rotations, turn_inverse
    ).reshape(PIXELS, -1)
    norms = jnp.sum(gathered * gathered, axis=0)
    group_hot = image_group[:, None] == jnp.arange(noise_var.shape[0])[None, :]
    sigma = jnp.sum(jnp.where(group_hot, noise_var[None, :], 0.0), axis=1)
    scores = (
        jnp.dot(
            images, rotated, precision=lax.Precision.HIGHEST, preferred_element_type=jnp.float32
        )
        - 0.5 * norms[None, :]
    ) / sigma[:, None]
    local_top = jnp.max(scores, axis=1)
    local_total = jnp.sum(jnp.exp(scores - local_top[:, None]), axis=1)
    top, total = joined((local_top, local_total), ("ref", "rep"), combine_stats)
    log_evidence = top + jnp.log(total)
    posterior = jnp.exp(scores - log_evidence[:, None])
    weight_sum = lax.psum(jnp.sum(posterior, axis=0), "img")
    numer_image = lax.dot_general(
        images,
        posterior,
        (((0,), (0,)), ((), ())),
        precision=lax.Precision.HIGHEST,
        preferred_element_type=jnp.float32,
    )
    numerator = select_turn(
        numer_image.reshape(IMAGE_SIDE, IMAGE_SIDE, -1), rotations, turn_forward
    ).reshape(PIXELS, -1)
    owned = lax.psum_scatter(numerator, "img", scatter_dimension=0, tiled=True)
    class_means = owned / (weight_sum + 1.0)[None, :]
    class_total = weight_sum.shape[0] * lax.axis_size("ref") * lax.axis_size("rep")
    image_total = images.shape[0] * lax.axis_size("img")
    class_weights = weight_sum * (class_total / image_total)
    return (class_means, class_weights, log_evidence)


def halves(x):
    high = x.astype(BF16)
    return high, (x - high.astype(F32)).astype(BF16)


def reverse_rows(x):
    place = lax.broadcasted_iota(jnp.int32, (8, x.shape[1]), 0)
    odd = place % 2 == 1
    second = (place // 2) % 2 == 1
    pieces = []
    for g in reversed(range(x.shape[0] // 8)):
        p = x[8 * g : 8 * g + 8]
        p = jnp.where(odd, pltpu.roll(p, 1, 0), pltpu.roll(p, 7, 0))
        p = jnp.where(second, pltpu.roll(p, 2, 0), pltpu.roll(p, 6, 0))
        pieces.append(pltpu.roll(p, 4, 0))
    return jnp.concatenate(pieces, axis=0)


def kernel(
    zs, weight_scale,
    images_ref, source_ref, rot_ref, group_ref, noise_ref,
    means_ref, weights_ref, evidence_ref,
    full, wide, scores, parts, stats, posts, num, refs_ref, factors, tall_high, tall_low, post_high, post_low,
    load_sem, refs_sem, z_recv, x_recv, cx_recv,
    right_send, left_send, x_send, cx_send,
    s_send, s_recv, t_send, t_recv, p_send, p_recv, f_send, f_recv,
):
    z = lax.axis_index("img")
    x = lax.axis_index("ref")
    c = lax.axis_index("rep")
    rows = images_ref.shape[0]
    classes = refs_ref.shape[1]
    quarter = rows // 4
    strip = PIXELS // CHUNKS
    side = IMAGE_SIDE
    own_lines = side // zs
    others = [{"ref": 1 - x}, {"rep": 1 - c}, {"ref": 1 - x, "rep": 1 - c}]

    load_refs = pltpu.make_async_copy(source_ref, refs_ref, refs_sem)
    load_refs.start()
    loads = [
        pltpu.make_async_copy(images_ref.at[:, chunk * strip : (chunk + 1) * strip], full.at[z, chunk], load_sem.at[chunk])
        for chunk in range(CHUNKS)
    ]
    for load in loads:
        load.start()
    barrier = pltpu.get_barrier_semaphore()
    for d in range(1, zs):
        pl.semaphore_signal(barrier, inc=1, device_id={"img": lax.rem(z + d, zs)}, device_id_type=MESH)
    for where in others:
        pl.semaphore_signal(barrier, inc=1, device_id=where, device_id_type=MESH)

    def clear(i, _):
        wide[:, pl.ds(pl.multiple_of(i * side, side), side), :] = jnp.zeros((classes // LANES, side, LANES), F32)
        return 0

    lax.fori_loop(0, side, clear, 0)
    for src in range(zs):
        post_high[src * LANES + rows : (src + 1) * LANES, :] = jnp.zeros((LANES - rows, classes), BF16)
        post_low[src * LANES + rows : (src + 1) * LANES, :] = jnp.zeros((LANES - rows, classes), BF16)
    pl.semaphore_wait(barrier, zs + 2)

    def quarter_rows(xi, ci):
        return pl.ds(pl.multiple_of((ci * 2 + xi) * quarter, 8), quarter)

    def columns(chunk):
        return pl.ds(pl.multiple_of(chunk * strip, strip), strip)

    def send(src, dst, ssem, rsem, where):
        return pltpu.make_async_remote_copy(
            src_ref=src, dst_ref=dst, send_sem=ssem, recv_sem=rsem,
            device_id=where, device_id_type=MESH,
        )

    def piece(src, chunk, xi, ci):
        return full.at[src, chunk, quarter_rows(xi, ci), :]

    def go_right(src, chunk, first=False):
        a = images_ref.at[quarter_rows(x, c), columns(chunk)] if first else piece(src, chunk, x, c)
        return send(a, piece(src, chunk, x, c), right_send.at[src, chunk], z_recv.at[src, chunk], {"img": lax.rem(z + 1, zs)})

    def go_left(src, chunk, first=False):
        a = images_ref.at[quarter_rows(x, c), columns(chunk)] if first else piece(src, chunk, x, c)
        return send(a, piece(src, chunk, x, c), left_send.at[src, chunk], z_recv.at[src, chunk], {"img": lax.rem(z + zs - 1, zs)})

    def go_x(src, chunk):
        return send(piece(src, chunk, x, c), piece(src, chunk, x, c), x_send.at[src, chunk], x_recv.at[src, chunk], {"ref": 1 - x})

    def go_cx(src, chunk):
        pair = full.at[src, chunk, pl.ds(pl.multiple_of(c * 2 * quarter, 8), 2 * quarter), :]
        return send(pair, pair, cx_send.at[src, chunk], cx_recv.at[src, chunk], {"rep": 1 - c})

    def partial(src):
        return send(scores.at[src], parts.at[z], s_send.at[src], s_recv.at[z], {"img": src})

    for chunk in range(CHUNKS):
        @pl.when(z < zs - 1)
        def _():
            go_right(z, chunk, True).start()

        @pl.when(z > 0)
        def _():
            go_left(z, chunk, True).start()

    rot = rot_ref[...]
    is_row = (rot == 0) | (rot == 7)
    is_row_up = (rot == 5) | (rot == 2)
    is_col = (rot == 4) | (rot == 3)
    is_col_up = (rot == 1) | (rot == 6)
    flipped = (rot == 7) | (rot == 2) | (rot == 3) | (rot == 6)

    def lane(h):
        return slice(h * LANES, (h + 1) * LANES)

    def line(i):
        return pl.ds(pl.multiple_of(i * side, side), side)

    def turned(i):
        field = refs_ref[line(i), :]
        return jnp.where(flipped, reverse_rows(field), field)

    def put_rows(i, norm):
        raw = refs_ref[line(i), :]
        field = turned(i)
        up = jnp.where(is_row, field, 0.0)
        down = jnp.where(is_row_up, field, 0.0)
        for h in range(classes // LANES):
            wide[h, line(z * own_lines + i), :] = up[:, lane(h)]
            wide[h, line(side - 1 - z * own_lines - i), :] = down[:, lane(h)]
        return norm + jnp.sum(raw * raw, axis=0, keepdims=True)

    def put_columns(i, _):
        field = turned(i)
        across = jnp.where(is_col, field, 0.0)
        back = jnp.where(is_col_up, field, 0.0)
        for h in range(classes // LANES):
            at = pl.ds(z * own_lines + i, side, stride=side)
            wide[h, at, :] = wide[h, at, :] + across[:, lane(h)]
            at = pl.ds(side - 1 - z * own_lines - i, side, stride=side)
            wide[h, at, :] = wide[h, at, :] + back[:, lane(h)]
        return 0

    def multiply(src, chunk):
        at = columns(chunk)
        weight = jnp.concatenate([wide[h, at, :] for h in range(classes // LANES)], axis=1)
        return jnp.dot(full[src, chunk], weight, precision=lax.Precision.HIGHEST, preferred_element_type=F32)

    def keep(src, chunk):
        block = full[src, chunk]
        if rows < LANES:
            block = jnp.concatenate([block, jnp.zeros((LANES - rows, strip), F32)], axis=0)
        high, low = halves(block.T)
        at = pl.ds(pl.multiple_of(src * LANES, LANES), LANES)
        tall_high[columns(chunk), at] = high
        tall_low[columns(chunk), at] = low

    def prepare_rows():
        load_refs.wait()
        norm = lax.fori_loop(0, own_lines, put_rows, jnp.zeros((1, classes), F32))
        start = jnp.broadcast_to(-0.5 * norm, (rows, classes))
        for src in range(zs):
            scores[src] = start
        for load in loads:
            load.wait()

    def own_part(chunk):
        scores[z] = scores[z] + multiply(z, chunk)
        keep(z, chunk)

    units = (zs - 1) * CHUNKS
    lead = max(CHUNKS, 4)

    def each(n, action):
        s = 1 + n // CHUNKS
        chunk = lax.rem(n, CHUNKS)
        good = (n >= 0) & (n < units)

        @pl.when(good & (z - s >= 0))
        def _():
            action(z - s, chunk, True)

        @pl.when(good & (z + s <= zs - 1))
        def _():
            action(z + s, chunk, False)

    def take_z(src, chunk, rightward):
        go_right(src, chunk).wait_recv()
        if rightward:
            @pl.when(z < zs - 1)
            def _():
                go_right(src, chunk).start()
        else:
            @pl.when(z > 0)
            def _():
                go_left(src, chunk).start()
        go_x(src, chunk).start()

    def take_x(src, chunk, rightward):
        go_x(src, chunk).wait_recv()
        go_cx(src, chunk).start()

    def take_all(src, chunk, rightward):
        go_cx(src, chunk).wait_recv()
        scores[src] = scores[src] + multiply(src, chunk)
        keep(src, chunk)

        @pl.when(chunk == CHUNKS - 1)
        def _():
            partial(src).start()

    def unit(n, _):
        each(n, take_z)
        each(n - 1, take_x)

        @pl.when(n == 0)
        def _():
            prepare_rows()

        @pl.when((n >= 1) & (n < lead // 2))
        def _():
            steps = lead // 2 - 1
            lax.fori_loop((n - 1) * own_lines // steps, n * own_lines // steps, put_columns, 0)

        for k in range(lead // 2, lead):
            @pl.when(n == k)
            def _():
                share = CHUNKS * 2 // lead
                for chunk in range((k - lead // 2) * share, (k - lead // 2 + 1) * share):
                    own_part(chunk)

        each(jnp.where(n < lead, -1, jnp.where(n < 2 * lead - 2, 2 * (n - lead), n - 2)), take_all)
        each(jnp.where((n < lead) | (n >= 2 * lead - 2), -1, 2 * (n - lead) + 1), take_all)
        return 0

    lax.fori_loop(0, units + 2, unit, 0)

    total_score = scores[z]
    for d in range(1, zs):
        src = lax.rem(z + d, zs)
        send(scores.at[src], parts.at[src], s_send.at[src], s_recv.at[src], {"img": src}).wait_recv()
        total_score = total_score + parts[src]
    groups = group_ref[...]
    sigma_row = jnp.zeros(groups.shape, F32)
    for g in range(noise_ref.shape[1]):
        sigma_row = jnp.where(groups == g, noise_ref[0:1, g : g + 1], sigma_row)

    def upright(row):
        return jnp.broadcast_to(row, (LANES, row.shape[1])).T[:, 0:1]

    total_score = total_score / upright(sigma_row)
    top = jnp.max(total_score, axis=1, keepdims=True)
    shifted = jnp.exp(total_score - top)
    posts[z] = shifted

    def give(src):
        return send(posts.at[z], posts.at[z], p_send.at[src], p_recv.at[z], {"img": src})

    def give_factor(src):
        return send(factors.at[z], factors.at[z], f_send.at[src], f_recv.at[z], {"img": src})

    for d in range(1, zs):
        give(lax.rem(z + d, zs)).start()
    total = jnp.sum(shifted, axis=1, keepdims=True)
    place = lax.broadcasted_iota(jnp.int32, (rows, LANES), 1)
    pair = jnp.where(place < LANES // 2, top, total)
    if rows < LANES:
        pair = jnp.concatenate([pair, jnp.ones((LANES - rows, LANES), F32)], axis=0)
    pair = pair.T
    tops, totals = pair[0:8], pair[LANES // 2 : LANES // 2 + 8]
    stats[3, 0:8, :] = tops
    stats[3, 8:16, :] = totals
    shares = [send(stats.at[3], stats.at[m], t_send.at[m], t_recv.at[m], where) for m, where in enumerate(others)]
    for share in shares:
        share.start()
    for share in shares:
        share.wait()
    best = tops
    for m in range(3):
        best = jnp.maximum(best, stats[m, 0:8, :])
    summed = totals * jnp.exp(tops - best)
    for m in range(3):
        summed = summed + stats[m, 8:16, :] * jnp.exp(stats[m, 0:8, :] - best)
    evidence = best + jnp.log(summed)
    evidence_ref[...] = evidence[0:1, :rows]
    factors[z] = jnp.exp(tops - evidence)
    for d in range(1, zs):
        give_factor(lax.rem(z + d, zs)).start()

    def settle_posts(src, weight_sum):
        factor = upright(factors[src, 0:1, :])[:rows]
        post = posts[src] * factor
        high, low = halves(post)
        at = pl.ds(pl.multiple_of(src * LANES, LANES), rows)
        post_high[at, :] = high
        post_low[at, :] = low
        return weight_sum + jnp.sum(post, axis=0, keepdims=True)

    weight_sum = settle_posts(z, jnp.zeros((1, classes), F32))
    for d in range(1, zs):
        src = lax.rem(z + d, zs)
        send(posts.at[src], posts.at[src], p_send.at[src], p_recv.at[src], {"img": src}).wait_recv()
        send(factors.at[src], factors.at[src], f_send.at[src], f_recv.at[src], {"img": src}).wait_recv()
        weight_sum = settle_posts(src, weight_sum)
    weights_ref[...] = weight_sum * weight_scale
    width = 512

    def weigh(n, _):
        at = pl.ds(pl.multiple_of(n * width, width), width)
        ah, al, bh, bl = tall_high[at, :], tall_low[at, :], post_high[...], post_low[...]
        one = lambda p, q: jnp.dot(p, q, preferred_element_type=F32)
        result = one(ah, bh) + (one(ah, bl) + one(al, bh))
        for h in range(classes // LANES):
            num[h, at, :] = result[:, lane(h)]
        return 0

    lax.fori_loop(0, PIXELS // width, weigh, 0)

    scale = 1.0 / (weight_sum + 1.0)

    def finish(i, _):
        fields = []
        for h in range(classes // LANES):
            up = num[h, line(z * own_lines + i), :]
            down = num[h, line(side - 1 - z * own_lines - i), :]
            across = num[h, pl.ds(z * own_lines + i, side, stride=side), :]
            back = num[h, pl.ds(side - 1 - z * own_lines - i, side, stride=side), :]
            k = lane(h)
            fields.append(jnp.where(is_row[:, k], up, jnp.where(is_row_up[:, k], down, jnp.where(is_col[:, k], across, back))))
        field = jnp.concatenate(fields, axis=1)
        means_ref[line(i), :] = jnp.where(flipped, reverse_rows(field), field) * scale
        return 0

    lax.fori_loop(0, own_lines, finish, 0)

    def settle(src, chunk, rightward):
        if rightward:
            @pl.when(z < zs - 1)
            def _():
                go_right(src, chunk).wait_send()
        else:
            @pl.when(z > 0)
            def _():
                go_left(src, chunk).wait_send()
        go_x(src, chunk).wait_send()
        go_cx(src, chunk).wait_send()

    def settle_unit(n, _):
        each(n, settle)
        return 0

    lax.fori_loop(0, units, settle_unit, 0)
    for chunk in range(CHUNKS):
        @pl.when(z < zs - 1)
        def _():
            go_right(z, chunk, True).wait_send()

        @pl.when(z > 0)
        def _():
            go_left(z, chunk, True).wait_send()
    for d in range(1, zs):
        src = lax.rem(z + d, zs)
        partial(src).wait_send()
        give(src).wait_send()
        give_factor(src).wait_send()


def turned_images_body(zs, images, references, rotations, image_group, noise_var):
    rows = images.shape[0]
    pixels, classes = references.shape
    class_total = classes * lax.axis_size("ref") * lax.axis_size("rep")
    image_total = rows * zs
    dma = pltpu.SemaphoreType.DMA
    vmem = pl.BlockSpec(memory_space=pltpu.VMEM)
    many = dma((zs, CHUNKS))
    means, weight_sum, evidence = pl.pallas_call(
        functools.partial(kernel, zs, class_total / image_total),
        name="class_step",
        out_shape=(
            jax.ShapeDtypeStruct((pixels, classes), F32),
            jax.ShapeDtypeStruct((1, classes), F32),
            jax.ShapeDtypeStruct((1, rows), F32),
        ),
        in_specs=[pl.BlockSpec(memory_space=pl.ANY), pl.BlockSpec(memory_space=pl.ANY), vmem, vmem, vmem],
        out_specs=(vmem, vmem, vmem),
        scratch_shapes=[
            pltpu.VMEM((zs, CHUNKS, rows, PIXELS // CHUNKS), F32),
            pltpu.VMEM((classes // LANES, PIXELS, LANES), F32),
            pltpu.VMEM((zs, rows, classes), F32),
            pltpu.VMEM((zs, rows, classes), F32),
            pltpu.VMEM((4, 16, LANES), F32),
            pltpu.VMEM((zs, rows, classes), F32),
            pltpu.VMEM((classes // LANES, PIXELS, LANES), F32),
            pltpu.VMEM((pixels, classes), F32),
            pltpu.VMEM((zs, 8, LANES), F32),
            pltpu.VMEM((PIXELS, zs * LANES), BF16),
            pltpu.VMEM((PIXELS, zs * LANES), BF16),
            pltpu.VMEM((zs * LANES, classes), BF16),
            pltpu.VMEM((zs * LANES, classes), BF16),
            dma((CHUNKS,)), dma, many, many, many, many, many, many, many,
            dma((zs,)), dma((zs,)), dma((3,)), dma((3,)), dma((zs,)), dma((zs,)), dma((zs,)), dma((zs,)),
        ],
        compiler_params=pltpu.CompilerParams(
            collective_id=0, has_side_effects=True, vmem_limit_bytes=VMEM_BYTES
        ),
    )(images, references, rotations[None, :], image_group[None, :], noise_var[None, :])
    return (means, weight_sum[0], evidence[0])


def solution(mesh):
    sizes = dict(mesh.shape)
    placed = (
        P(("groups", "img"), None),
        P("img", ("groups", "ref", "rep")),
        P(("groups", "ref", "rep")),
        P(("groups", "img")),
        P(),
    )

    def choose(images, references, rotations, image_group, noise_var):
        zs = sizes["img"]
        rows = images.shape[0]
        fits = (
            sizes["ref"] == 2
            and sizes["rep"] == 2
            and zs % 2 == 0
            and rows % 32 == 0
            and rows <= LANES
            and zs >= 4
            and references.shape[1] % LANES == 0
            and IMAGE_SIDE % zs == 0
            and zs * rows * PIXELS * 4 <= 12 * 1024 * 1024
        )
        if fits:
            return turned_images_body(zs, images, references, rotations, image_group, noise_var)
        return body(images, references, rotations, image_group, noise_var)

    return jax.shard_map(
        choose,
        mesh=mesh,
        in_specs=placed,
        out_specs=(
            P("img", ("groups", "ref", "rep")),
            P(("groups", "ref", "rep")),
            P(("groups", "img")),
        ),
        check_vma=False,
    )
```

```python
import functools

import jax
import jax.numpy as jnp
from jax import lax
from jax.experimental import pallas as pl
from jax.experimental.pallas import tpu as pltpu
from jax.sharding import PartitionSpec as P

IMAGE_SIDE = 64
PIXELS = 4096
MESH = pl.DeviceIdType.MESH
F32 = jnp.float32
BF16 = jnp.bfloat16
CHUNKS = 2
LANES = 128
VMEM_BYTES = 62 * 1024 * 1024


def joined(part, axis, combine):
    gathered = jax.tree.map(lambda a: lax.all_gather(a, axis), part)

    def take(source):
        return jax.tree.map(lambda a: lax.dynamic_index_in_dim(a, source, 0, False), gathered)

    return lax.fori_loop(
        1, lax.axis_size(axis), lambda source, state: combine(state, take(source)), take(0)
    )


def turn_forward(field, which):
    quarter = which % 4
    base = field if which < 4 else jnp.swapaxes(field, 0, 1)
    return jnp.rot90(base, quarter, axes=(0, 1))


def turn_inverse(field, which):
    quarter = which % 4
    base = jnp.rot90(field, -quarter, axes=(0, 1))
    return base if which < 4 else jnp.swapaxes(base, 0, 1)


def select_turn(field, rotations, turner):
    result = jnp.zeros_like(field)
    for which in range(8):
        result = jnp.where(rotations[None, None, :] == which, turner(field, which), result)
    return result


def combine_stats(first, second):
    top = jnp.maximum(first[0], second[0])
    total = first[1] * jnp.exp(first[0] - top) + second[1] * jnp.exp(second[0] - top)
    return (top, total)


def body(images, references, rotations, image_group, noise_var):
    gathered = lax.all_gather(references, "img", axis=0, tiled=True)
    rotated = select_turn(
        gathered.reshape(IMAGE_SIDE, IMAGE_SIDE, -1), rotations, turn_inverse
    ).reshape(PIXELS, -1)
    norms = jnp.sum(gathered * gathered, axis=0)
    group_hot = image_group[:, None] == jnp.arange(noise_var.shape[0])[None, :]
    sigma = jnp.sum(jnp.where(group_hot, noise_var[None, :], 0.0), axis=1)
    scores = (
        jnp.dot(
            images, rotated, precision=lax.Precision.HIGHEST, preferred_element_type=jnp.float32
        )
        - 0.5 * norms[None, :]
    ) / sigma[:, None]
    local_top = jnp.max(scores, axis=1)
    local_total = jnp.sum(jnp.exp(scores - local_top[:, None]), axis=1)
    top, total = joined((local_top, local_total), ("ref", "rep"), combine_stats)
    log_evidence = top + jnp.log(total)
    posterior = jnp.exp(scores - log_evidence[:, None])
    weight_sum = lax.psum(jnp.sum(posterior, axis=0), "img")
    numer_image = lax.dot_general(
        images,
        posterior,
        (((0,), (0,)), ((), ())),
        precision=lax.Precision.HIGHEST,
        preferred_element_type=jnp.float32,
    )
    numerator = select_turn(
        numer_image.reshape(IMAGE_SIDE, IMAGE_SIDE, -1), rotations, turn_forward
    ).reshape(PIXELS, -1)
    owned = lax.psum_scatter(numerator, "img", scatter_dimension=0, tiled=True)
    class_means = owned / (weight_sum + 1.0)[None, :]
    class_total = weight_sum.shape[0] * lax.axis_size("ref") * lax.axis_size("rep")
    image_total = images.shape[0] * lax.axis_size("img")
    class_weights = weight_sum * (class_total / image_total)
    return (class_means, class_weights, log_evidence)


def halves(x):
    high = x.astype(BF16)
    return high, (x - high.astype(F32)).astype(BF16)


def reverse_rows(x):
    place = lax.broadcasted_iota(jnp.int32, (8, x.shape[1]), 0)
    odd = place % 2 == 1
    second = (place // 2) % 2 == 1
    pieces = []
    for g in reversed(range(x.shape[0] // 8)):
        p = x[8 * g : 8 * g + 8]
        p = jnp.where(odd, pltpu.roll(p, 1, 0), pltpu.roll(p, 7, 0))
        p = jnp.where(second, pltpu.roll(p, 2, 0), pltpu.roll(p, 6, 0))
        pieces.append(pltpu.roll(p, 4, 0))
    return jnp.concatenate(pieces, axis=0)


def kernel(
    zs, weight_scale,
    images_ref, source_ref, rot_ref, group_ref, noise_ref,
    means_ref, weights_ref, evidence_ref,
    full, wide, scores, parts, stats, posts, num, refs_ref, factors, tall_high, tall_low, post_high, post_low,
    load_sem, refs_sem, z_recv, x_recv, cx_recv,
    right_send, left_send, x_send, cx_send,
    s_send, s_recv, t_send, t_recv, p_send, p_recv, f_send, f_recv,
):
    z = lax.axis_index("img")
    x = lax.axis_index("ref")
    c = lax.axis_index("rep")
    rows = images_ref.shape[0]
    classes = refs_ref.shape[1]
    quarter = rows // 4
    strip = PIXELS // CHUNKS
    side = IMAGE_SIDE
    own_lines = side // zs
    others = [{"ref": 1 - x}, {"rep": 1 - c}, {"ref": 1 - x, "rep": 1 - c}]

    load_refs = pltpu.make_async_copy(source_ref, refs_ref, refs_sem)
    load_refs.start()
    loads = [
        pltpu.make_async_copy(images_ref.at[:, chunk * strip : (chunk + 1) * strip], full.at[z, chunk], load_sem.at[chunk])
        for chunk in range(CHUNKS)
    ]
    for load in loads:
        load.start()
    barrier = pltpu.get_barrier_semaphore()
    for d in range(1, zs):
        pl.semaphore_signal(barrier, inc=1, device_id={"img": lax.rem(z + d, zs)}, device_id_type=MESH)
    for where in others:
        pl.semaphore_signal(barrier, inc=1, device_id=where, device_id_type=MESH)

    def clear(i, _):
        wide[:, pl.ds(pl.multiple_of(i * side, side), side), :] = jnp.zeros((classes // LANES, side, LANES), F32)
        return 0

    lax.fori_loop(0, side, clear, 0)
    for src in range(zs):
        post_high[src * LANES + rows : (src + 1) * LANES, :] = jnp.zeros((LANES - rows, classes), BF16)
        post_low[src * LANES + rows : (src + 1) * LANES, :] = jnp.zeros((LANES - rows, classes), BF16)
    pl.semaphore_wait(barrier, zs + 2)

    def quarter_rows(xi, ci):
        return pl.ds(pl.multiple_of((ci * 2 + xi) * quarter, 8), quarter)

    def columns(chunk):
        return pl.ds(pl.multiple_of(chunk * strip, strip), strip)

    def send(src, dst, ssem, rsem, where):
        return pltpu.make_async_remote_copy(
            src_ref=src, dst_ref=dst, send_sem=ssem, recv_sem=rsem,
            device_id=where, device_id_type=MESH,
        )

    def piece(src, chunk, xi, ci):
        return full.at[src, chunk, quarter_rows(xi, ci), :]

    def go_right(src, chunk, first=False):
        a = images_ref.at[quarter_rows(x, c), columns(chunk)] if first else piece(src, chunk, x, c)
        return send(a, piece(src, chunk, x, c), right_send.at[src, chunk], z_recv.at[src, chunk], {"img": lax.rem(z + 1, zs)})

    def go_left(src, chunk, first=False):
        a = images_ref.at[quarter_rows(x, c), columns(chunk)] if first else piece(src, chunk, x, c)
        return send(a, piece(src, chunk, x, c), left_send.at[src, chunk], z_recv.at[src, chunk], {"img": lax.rem(z + zs - 1, zs)})

    def go_x(src, chunk):
        return send(piece(src, chunk, x, c), piece(src, chunk, x, c), x_send.at[src, chunk], x_recv.at[src, chunk], {"ref": 1 - x})

    def go_cx(src, chunk):
        pair = full.at[src, chunk, pl.ds(pl.multiple_of(c * 2 * quarter, 8), 2 * quarter), :]
        return send(pair, pair, cx_send.at[src, chunk], cx_recv.at[src, chunk], {"rep": 1 - c})

    def partial(src):
        return send(scores.at[src], parts.at[z], s_send.at[src], s_recv.at[z], {"img": src})

    for chunk in range(CHUNKS):
        @pl.when(z < zs - 1)
        def _():
            go_right(z, chunk, True).start()

        @pl.when(z > 0)
        def _():
            go_left(z, chunk, True).start()

    rot = rot_ref[...]
    is_row = (rot == 0) | (rot == 7)
    is_row_up = (rot == 5) | (rot == 2)
    is_col = (rot == 4) | (rot == 3)
    is_col_up = (rot == 1) | (rot == 6)
    flipped = (rot == 7) | (rot == 2) | (rot == 3) | (rot == 6)

    def lane(h):
        return slice(h * LANES, (h + 1) * LANES)

    def line(i):
        return pl.ds(pl.multiple_of(i * side, side), side)

    def turned(i):
        field = refs_ref[line(i), :]
        return jnp.where(flipped, reverse_rows(field), field)

    def put_rows(i, norm):
        raw = refs_ref[line(i), :]
        field = turned(i)
        up = jnp.where(is_row, field, 0.0)
        down = jnp.where(is_row_up, field, 0.0)
        for h in range(classes // LANES):
            wide[h, line(z * own_lines + i), :] = up[:, lane(h)]
            wide[h, line(side - 1 - z * own_lines - i), :] = down[:, lane(h)]
        return norm + jnp.sum(raw * raw, axis=0, keepdims=True)

    def put_columns(i, _):
        field = turned(i)
        across = jnp.where(is_col, field, 0.0)
        back = jnp.where(is_col_up, field, 0.0)
        for h in range(classes // LANES):
            at = pl.ds(z * own_lines + i, side, stride=side)
            wide[h, at, :] = wide[h, at, :] + across[:, lane(h)]
            at = pl.ds(side - 1 - z * own_lines - i, side, stride=side)
            wide[h, at, :] = wide[h, at, :] + back[:, lane(h)]
        return 0

    def multiply(src, chunk):
        at = columns(chunk)
        weight = jnp.concatenate([wide[h, at, :] for h in range(classes // LANES)], axis=1)
        return jnp.dot(full[src, chunk], weight, precision=lax.Precision.HIGHEST, preferred_element_type=F32)

    def keep(src, chunk):
        block = full[src, chunk]
        if rows < LANES:
            block = jnp.concatenate([block, jnp.zeros((LANES - rows, strip), F32)], axis=0)
        high, low = halves(block.T)
        at = pl.ds(pl.multiple_of(src * LANES, LANES), LANES)
        tall_high[columns(chunk), at] = high
        tall_low[columns(chunk), at] = low

    def prepare_rows():
        load_refs.wait()
        norm = lax.fori_loop(0, own_lines, put_rows, jnp.zeros((1, classes), F32))
        start = jnp.broadcast_to(-0.5 * norm, (rows, classes))
        for src in range(zs):
            scores[src] = start
        for load in loads:
            load.wait()

    def own_part(chunk):
        scores[z] = scores[z] + multiply(z, chunk)
        keep(z, chunk)

    units = (zs - 1) * CHUNKS
    lead = max(CHUNKS, 4)

    def each(n, action):
        s = 1 + n // CHUNKS
        chunk = lax.rem(n, CHUNKS)
        good = (n >= 0) & (n < units)

        @pl.when(good & (z - s >= 0))
        def _():
            action(z - s, chunk, True)

        @pl.when(good & (z + s <= zs - 1))
        def _():
            action(z + s, chunk, False)

    def take_z(src, chunk, rightward):
        go_right(src, chunk).wait_recv()
        if rightward:
            @pl.when(z < zs - 1)
            def _():
                go_right(src, chunk).start()
        else:
            @pl.when(z > 0)
            def _():
                go_left(src, chunk).start()
        go_x(src, chunk).start()

    def take_x(src, chunk, rightward):
        go_x(src, chunk).wait_recv()
        go_cx(src, chunk).start()

    def take_all(src, chunk, rightward):
        go_cx(src, chunk).wait_recv()
        scores[src] = scores[src] + multiply(src, chunk)
        keep(src, chunk)

        @pl.when(chunk == CHUNKS - 1)
        def _():
            partial(src).start()

    def unit(n, _):
        each(n, take_z)
        each(n - 1, take_x)

        @pl.when(n == 0)
        def _():
            prepare_rows()

        @pl.when((n >= 1) & (n < lead // 2))
        def _():
            steps = lead // 2 - 1
            lax.fori_loop((n - 1) * own_lines // steps, n * own_lines // steps, put_columns, 0)

        for k in range(lead // 2, lead):
            @pl.when(n == k)
            def _():
                share = CHUNKS * 2 // lead
                for chunk in range((k - lead // 2) * share, (k - lead // 2 + 1) * share):
                    own_part(chunk)

        each(jnp.where(n < lead, -1, jnp.where(n < 2 * lead - 2, 2 * (n - lead), n - 2)), take_all)
        each(jnp.where((n < lead) | (n >= 2 * lead - 2), -1, 2 * (n - lead) + 1), take_all)
        return 0

    lax.fori_loop(0, units + 2, unit, 0)

    total_score = scores[z]
    for d in range(1, zs):
        src = lax.rem(z + d, zs)
        send(scores.at[src], parts.at[src], s_send.at[src], s_recv.at[src], {"img": src}).wait_recv()
        total_score = total_score + parts[src]
    groups = group_ref[...]
    sigma_row = jnp.zeros(groups.shape, F32)
    for g in range(noise_ref.shape[1]):
        sigma_row = jnp.where(groups == g, noise_ref[0:1, g : g + 1], sigma_row)

    def upright(row):
        return jnp.broadcast_to(row, (LANES, row.shape[1])).T[:, 0:1]

    total_score = total_score / upright(sigma_row)
    top = jnp.max(total_score, axis=1, keepdims=True)
    shifted = jnp.exp(total_score - top)
    posts[z] = shifted

    def give(src):
        return send(posts.at[z], posts.at[z], p_send.at[src], p_recv.at[z], {"img": src})

    def give_factor(src):
        return send(factors.at[z], factors.at[z], f_send.at[src], f_recv.at[z], {"img": src})

    for d in range(1, zs):
        give(lax.rem(z + d, zs)).start()
    total = jnp.sum(shifted, axis=1, keepdims=True)
    place = lax.broadcasted_iota(jnp.int32, (rows, LANES), 1)
    pair = jnp.where(place < LANES // 2, top, total)
    if rows < LANES:
        pair = jnp.concatenate([pair, jnp.ones((LANES - rows, LANES), F32)], axis=0)
    pair = pair.T
    tops, totals = pair[0:8], pair[LANES // 2 : LANES // 2 + 8]
    stats[3, 0:8, :] = tops
    stats[3, 8:16, :] = totals
    shares = [send(stats.at[3], stats.at[m], t_send.at[m], t_recv.at[m], where) for m, where in enumerate(others)]
    for share in shares:
        share.start()
    for share in shares:
        share.wait()
    best = tops
    for m in range(3):
        best = jnp.maximum(best, stats[m, 0:8, :])
    summed = totals * jnp.exp(tops - best)
    for m in range(3):
        summed = summed + stats[m, 8:16, :] * jnp.exp(stats[m, 0:8, :] - best)
    evidence = best + jnp.log(summed)
    evidence_ref[...] = evidence[0:1, :rows]
    factors[z] = jnp.exp(tops - evidence)
    for d in range(1, zs):
        give_factor(lax.rem(z + d, zs)).start()

    def settle_posts(src, weight_sum):
        factor = upright(factors[src, 0:1, :])[:rows]
        post = posts[src] * factor
        high, low = halves(post)
        at = pl.ds(pl.multiple_of(src * LANES, LANES), rows)
        post_high[at, :] = high
        post_low[at, :] = low
        return weight_sum + jnp.sum(post, axis=0, keepdims=True)

    weight_sum = settle_posts(z, jnp.zeros((1, classes), F32))
    for d in range(1, zs):
        src = lax.rem(z + d, zs)
        send(posts.at[src], posts.at[src], p_send.at[src], p_recv.at[src], {"img": src}).wait_recv()
        send(factors.at[src], factors.at[src], f_send.at[src], f_recv.at[src], {"img": src}).wait_recv()
        weight_sum = settle_posts(src, weight_sum)
    weights_ref[...] = weight_sum * weight_scale
    width = 1024

    def weigh(n, _):
        at = pl.ds(pl.multiple_of(n * width, width), width)
        ah, al, bh, bl = tall_high[at, :], tall_low[at, :], post_high[...], post_low[...]
        one = lambda p, q: jnp.dot(p, q, preferred_element_type=F32)
        result = one(ah, bh) + (one(ah, bl) + one(al, bh))
        for h in range(classes // LANES):
            num[h, at, :] = result[:, lane(h)]
        return 0

    lax.fori_loop(0, PIXELS // width, weigh, 0)

    scale = 1.0 / (weight_sum + 1.0)

    def finish(i, _):
        fields = []
        for h in range(classes // LANES):
            up = num[h, line(z * own_lines + i), :]
            down = num[h, line(side - 1 - z * own_lines - i), :]
            across = num[h, pl.ds(z * own_lines + i, side, stride=side), :]
            back = num[h, pl.ds(side - 1 - z * own_lines - i, side, stride=side), :]
            k = lane(h)
            fields.append(jnp.where(is_row[:, k], up, jnp.where(is_row_up[:, k], down, jnp.where(is_col[:, k], across, back))))
        field = jnp.concatenate(fields, axis=1)
        means_ref[line(i), :] = jnp.where(flipped, reverse_rows(field), field) * scale
        return 0

    lax.fori_loop(0, own_lines, finish, 0, unroll=2)

    def settle(src, chunk, rightward):
        if rightward:
            @pl.when(z < zs - 1)
            def _():
                go_right(src, chunk).wait_send()
        else:
            @pl.when(z > 0)
            def _():
                go_left(src, chunk).wait_send()
        go_x(src, chunk).wait_send()
        go_cx(src, chunk).wait_send()

    def settle_unit(n, _):
        each(n, settle)
        return 0

    lax.fori_loop(0, units, settle_unit, 0)
    for chunk in range(CHUNKS):
        @pl.when(z < zs - 1)
        def _():
            go_right(z, chunk, True).wait_send()

        @pl.when(z > 0)
        def _():
            go_left(z, chunk, True).wait_send()
    for d in range(1, zs):
        src = lax.rem(z + d, zs)
        partial(src).wait_send()
        give(src).wait_send()
        give_factor(src).wait_send()


def turned_images_body(zs, images, references, rotations, image_group, noise_var):
    rows = images.shape[0]
    pixels, classes = references.shape
    class_total = classes * lax.axis_size("ref") * lax.axis_size("rep")
    image_total = rows * zs
    dma = pltpu.SemaphoreType.DMA
    vmem = pl.BlockSpec(memory_space=pltpu.VMEM)
    many = dma((zs, CHUNKS))
    means, weight_sum, evidence = pl.pallas_call(
        functools.partial(kernel, zs, class_total / image_total),
        name="class_step",
        out_shape=(
            jax.ShapeDtypeStruct((pixels, classes), F32),
            jax.ShapeDtypeStruct((1, classes), F32),
            jax.ShapeDtypeStruct((1, rows), F32),
        ),
        in_specs=[pl.BlockSpec(memory_space=pl.ANY), pl.BlockSpec(memory_space=pl.ANY), vmem, vmem, vmem],
        out_specs=(vmem, vmem, vmem),
        scratch_shapes=[
            pltpu.VMEM((zs, CHUNKS, rows, PIXELS // CHUNKS), F32),
            pltpu.VMEM((classes // LANES, PIXELS, LANES), F32),
            pltpu.VMEM((zs, rows, classes), F32),
            pltpu.VMEM((zs, rows, classes), F32),
            pltpu.VMEM((4, 16, LANES), F32),
            pltpu.VMEM((zs, rows, classes), F32),
            pltpu.VMEM((classes // LANES, PIXELS, LANES), F32),
            pltpu.VMEM((pixels, classes), F32),
            pltpu.VMEM((zs, 8, LANES), F32),
            pltpu.VMEM((PIXELS, zs * LANES), BF16),
            pltpu.VMEM((PIXELS, zs * LANES), BF16),
            pltpu.VMEM((zs * LANES, classes), BF16),
            pltpu.VMEM((zs * LANES, classes), BF16),
            dma((CHUNKS,)), dma, many, many, many, many, many, many, many,
            dma((zs,)), dma((zs,)), dma((3,)), dma((3,)), dma((zs,)), dma((zs,)), dma((zs,)), dma((zs,)),
        ],
        compiler_params=pltpu.CompilerParams(
            collective_id=0, has_side_effects=True, vmem_limit_bytes=VMEM_BYTES
        ),
    )(images, references, rotations[None, :], image_group[None, :], noise_var[None, :])
    return (means, weight_sum[0], evidence[0])


def solution(mesh):
    sizes = dict(mesh.shape)
    placed = (
        P(("groups", "img"), None),
        P("img", ("groups", "ref", "rep")),
        P(("groups", "ref", "rep")),
        P(("groups", "img")),
        P(),
    )

    def choose(images, references, rotations, image_group, noise_var):
        zs = sizes["img"]
        rows = images.shape[0]
        fits = (
            sizes["ref"] == 2
            and sizes["rep"] == 2
            and zs % 2 == 0
            and rows % 32 == 0
            and rows <= LANES
            and zs >= 4
            and references.shape[1] % LANES == 0
            and IMAGE_SIDE % zs == 0
            and zs * rows * PIXELS * 4 <= 12 * 1024 * 1024
        )
        if fits:
            return turned_images_body(zs, images, references, rotations, image_group, noise_var)
        return body(images, references, rotations, image_group, noise_var)

    return jax.shard_map(
        choose,
        mesh=mesh,
        in_specs=placed,
        out_specs=(
            P("img", ("groups", "ref", "rep")),
            P(("groups", "ref", "rep")),
            P(("groups", "img")),
        ),
        check_vma=False,
    )
```
